32 devices in a mesh: scen: 2 (over x), tm: 16 (over z, y, core).
Axes of the slice: x: 2, y: 2, z: 4, core: 2. Of those that a mesh axis runs over, the one named last changes fastest.
Arguments:
- base_injection: bfloat16 [32, 36864], P(('scen', 'tm')), parts along dimension 0, may hold values from -6 to 6
- ptdf_tiles: bfloat16 [128, 80, 128, 128], P(None, 'tm'), may hold values from -0.0625 to 0.0625
- tile_block: int32 [128, 80], P(None, 'tm'), may hold values from 0 to 17
- limits: float32 [16384], replicated, may hold values from 0.5 to 2
- stor_bus: int32 [2048], replicated, may hold values from 0 to 36863
- stor_gain: float32 [2048], replicated, may hold values from 0.5 to 4
- soc_init: float32 [32, 2048], P(('scen', 'tm')), parts along dimension 0, may hold values from 0 to 1
Outputs:
- injection: float32 [32, 36864], P(('scen', 'tm')), parts along dimension 0
- line_dual: float32 [32, 16384], P(('scen', 'tm')), parts along dimension 0
- level: float32 [32, 2048], P(('scen', 'tm')), parts along dimension 0
The draws below stay inside these ranges and needn't reach their ends.
There are 2 independent parts, one for each index of `scen`. The reference program is written for one: setup_inputs(seed, part) draws one part's arguments, and reference() takes and returns one part's arrays. A program takes and returns all parts, laid end to end along the dimension named above; an argument that names none is the same for every part. Nothing has to cross between parts.
All inputs are finite; a program needn't handle non-finite values.
Results may differ from the reference program's by a relative error of at most 0.012.
The reference program's roundings to bfloat16 on the way count: a program that leaves them out, or rounds other values in their place, can miss the bound.
Values may be sent and summed in bfloat16 or wider, within the bound.
A program may use at most 128 MiB of HBM per device.

```python
import math
import jax
import jax.numpy as jnp
from jax import lax

TILE = 128
LG = 128
BB_DEV = 18
KD = 5
STOR = 2048
ITERS = 2
HOURS = 16
LINES = 16384
BUSES = 36864
N_TM = 16


def with_ends(values, own_key, least, high):
    index_at = [jax.random.randint(jax.random.fold_in(own_key, axis), (), 0, length) for axis, length in enumerate(values.shape)]
    longest = values.shape.index(max(values.shape))
    next_to = index_at[:longest] + [(index_at[longest] + 1) % values.shape[longest]] + index_at[longest + 1:]
    return values.at[tuple(index_at)].set(least).at[tuple(next_to)].set(high)


def block_levels(own_key, extent, pieces, low, largest):
    def one(dim, parts):
        draws = jax.random.uniform(jax.random.fold_in(jax.random.fold_in(own_key, 6), dim), (parts,), jnp.float32, low / len(pieces), largest / len(pieces))
        return jnp.repeat(jnp.exp(draws), extent[dim] // parts).reshape((-1,) + (1,) * (len(extent) - dim - 1))

    level = one(*pieces[0])
    for cut in pieces[1:]:
        level = level * one(*cut)
    return level


def centred(stream_key, dims, scale, reach, shards=(), kind=jnp.bfloat16):
    entries = jax.random.normal(stream_key, dims, jnp.float32) * scale
    if len(shards) > 0:
        entries = block_levels(stream_key, dims, shards, -0.22, 0.18) * entries
    return jnp.clip(entries, min=-reach, max=reach).astype(kind)


def setup_inputs(seed: int = 0, part: int = 0) -> dict:
    splits = jax.random.split(jax.random.key(seed), 8)
    own_keys = jax.random.split(jax.random.fold_in(splits[7], part), 8)
    return {
        "base_injection": centred(own_keys[0], (HOURS, BUSES), 1.0, 6.0, ((0, 16),)),
        "ptdf_tiles": centred(splits[1], (LG, KD * N_TM, TILE, TILE), (KD * N_TM * TILE) ** -0.5, 0.0625, ((1, 16),)),
        "tile_block": with_ends(jax.random.randint(splits[2], (LG, KD * N_TM), 0, BB_DEV), jax.random.fold_in(splits[2], 1), 0, BB_DEV - 1).astype(jnp.int32),
        "limits": jnp.clip(jax.random.uniform(splits[3], (LINES,), jnp.float32, 0.5, 2.0), 0.5, 2.0),
        "stor_bus": with_ends(jax.random.randint(splits[4], (STOR,), 0, BUSES), jax.random.fold_in(splits[4], 1), 0, BUSES - 1).astype(jnp.int32),
        "stor_gain": jnp.clip(jnp.exp(jax.random.uniform(splits[5], (STOR,), jnp.float32, math.log(0.5), math.log(4.0))), 0.5, 4.0),
        "soc_init": jnp.clip(1.0 * jax.random.uniform(own_keys[6], (HOURS, STOR), jnp.float32) ** block_levels(own_keys[6], (HOURS, STOR), ((0, 16),), -0.2, 0.2), 0.0, 1.0),
    }


step_size = 0.5
penalty = 4.0
ramp_weight = 0.5


def flow_product(sent, ptdf_tiles, tile_block):
    grid = sent.astype(jnp.float32).reshape(HOURS, N_TM, BB_DEV, TILE)
    tiles = ptdf_tiles.reshape(LG, N_TM, KD, TILE, TILE)
    blocks = tile_block.reshape(LG, N_TM, KD)
    device_ids = jnp.arange(N_TM, dtype=jnp.int32)[:, None]

    def one_group(pair):
        tiles_g, blocks_g = pair
        picked = grid[:, device_ids, blocks_g]
        return jnp.einsum("hnkb,nklb->hl", picked, tiles_g.astype(jnp.float32), precision=lax.Precision.HIGHEST)

    result = lax.map(one_group, (tiles, blocks))
    return jnp.transpose(result, (1, 0, 2)).reshape(HOURS, LG * TILE)


def price_product(dual_b, ptdf_tiles, tile_block):
    folded = jnp.transpose(dual_b.astype(jnp.float32).reshape(HOURS, LG, TILE), (1, 0, 2))
    tiles = ptdf_tiles.reshape(LG, N_TM, KD, TILE, TILE)
    blocks = tile_block.reshape(LG, N_TM, KD)
    device_ids = jnp.arange(N_TM, dtype=jnp.int32)[:, None]

    def add_group(total, triple):
        rows_g, tiles_g, blocks_g = triple
        contrib = jnp.einsum("hl,nklb->hnkb", rows_g, tiles_g.astype(jnp.float32), precision=lax.Precision.HIGHEST)
        return total.at[:, device_ids, blocks_g].add(contrib), None

    start_total = jnp.zeros((HOURS, N_TM, BB_DEV, TILE), jnp.float32)
    total, unused = lax.scan(add_group, start_total, (folded, tiles, blocks))
    return total.reshape(HOURS, BB_DEV * TILE * N_TM)


def reference(base_injection, ptdf_tiles, tile_block, limits, stor_bus, stor_gain, soc_init):
    base_full = base_injection.astype(jnp.float32)
    inject = base_full
    line_dual = jnp.zeros((HOURS, LG * TILE), jnp.float32)
    level = soc_init
    for iteration in range(ITERS):
        prev_inj = jnp.roll(inject, 1, axis=0)
        next_inj = jnp.roll(inject, -1, axis=0)
        prev_level = jnp.roll(level, 1, axis=0)
        line_flows = flow_product(inject.astype(jnp.bfloat16), ptdf_tiles, tile_block)
        shifted = line_flows + line_dual
        clipped = jnp.clip(shifted, -limits, limits)
        line_dual = shifted - clipped
        bus_price = price_product(line_dual.astype(jnp.bfloat16), ptdf_tiles, tile_block)
        store_price = bus_price[:, stor_bus]
        charge = level - prev_level
        updated = inject - step_size * ((inject - base_full) + penalty * bus_price
                                        + ramp_weight * (2.0 * inject - prev_inj - next_inj))
        updated = updated.at[:, stor_bus].add(-step_size * charge)
        level = 0.5 * (level + prev_level) - stor_gain * store_price
        inject = updated
    return inject, line_dual, level
```

```python
import functools

import jax
import jax.numpy as jnp
from jax import lax
from jax.experimental import pallas as pl
from jax.experimental.pallas import tpu as pltpu
from jax.sharding import PartitionSpec as P

ITERS = 2

step_size = 0.5
penalty = 4.0
ramp_weight = 0.5

VM = pl.BlockSpec(memory_space=pltpu.VMEM)
MESH = pl.DeviceIdType.MESH


def admm_kernel(
    n, unit_chunk, block_ref, block_rows_ref, base_row_ref, limits_ref, bus_ref, gain_ref, soc_ref, tiles_ref,
    inj_out, dual_out, level_out,
    held, rows, base, inj, sent, price, level_recv, level, pointers, table,
    theirs, mine, first_recv, first_sum, second_recv, own, all_dual, slots,
    inj_rows, dual_rows, level_rows, level_parts, level_last,
    tile_sem, table_sem, start_send, start_recv, pair_send, pair_recv, row_send, row_recv,
    far_send, far_recv, mid_send, mid_recv, near_send, near_recv, end_send, end_recv,
):
    half, quarter = n // 2, n // 4
    groups, depth, _, width = held.shape
    blocks, hours = base.shape[:2]
    reach = blocks * width
    own_groups = groups // n
    span = own_groups * width
    units = level.shape[1]
    me = lax.axis_index("tm")
    core = lax.rem(me, 2)
    side = lax.rem(me // 2, 2)
    spot = me // 2
    far, lane = me // 4, lax.rem(me, 4)
    partner = me + 1 - 2 * core
    across = me + 2 - 4 * side
    everyone = [lax.rem(me + k, n) for k in range(1, n)]

    def remote(src, dst, send, recv, device):
        return pltpu.make_async_remote_copy(
            src_ref=src, dst_ref=dst, send_sem=send, recv_sem=recv,
            device_id={"tm": device}, device_id_type=MESH,
        )

    def owner(k, other):
        return lax.rem(spot + k + 1, half) * 2 + (1 - core if other else core)

    def fetch(k, other):
        place = pl.ds(owner(k, other) * own_groups, own_groups)
        return pltpu.make_async_copy(
            tiles_ref.at[place], held.at[place], tile_sem.at[2 * k + (0 if other else 1)]
        )

    def chunk_at(pos):
        z = lax.rem(far + quarter - lax.rem(pos, quarter), quarter)
        y = lax.rem(side + lax.rem(pos // quarter, 2), 2)
        c = lax.rem(core + pos // half, 2)
        return z * 4 + y * 2 + c

    for k in range(half):
        fetch(k, True).start()
        fetch(k, False).start()

    barrier = pltpu.get_barrier_semaphore()
    for other in everyone:
        pl.semaphore_signal(barrier, inc=1, device_id={"tm": other}, device_id_type=MESH)

    group_pos = []
    for dim in (0, 1):
        g = lax.broadcasted_iota(jnp.int32, (groups, groups), dim)
        dev = lax.div(g, own_groups)
        turn = lax.rem(far + quarter - lax.div(dev, 4), quarter)
        other_side = lax.rem(lax.rem(lax.div(dev, 2), 2) + side, 2)
        other_core = lax.rem(lax.rem(dev, 2) + core, 2)
        pos = (other_core * half + other_side * quarter + turn) * own_groups + lax.rem(g, own_groups)
        group_pos.append(pos)
    down, along = group_pos
    numbers = lax.broadcasted_iota(jnp.int32, (groups, groups), 1)
    for k in range(depth):
        here = jnp.broadcast_to(block_rows_ref[k:k + 1, :], (groups, groups))
        there = here.T
        before = jnp.where((here == there) & (down < along), down + 1, 0)
        pointers[k:k + 1, :] = jnp.max(before, axis=0, keepdims=True)
        final = jnp.where(there == numbers, down + 1, 0)
        pointers[depth + k:depth + k + 1, :] = jnp.max(final, axis=0, keepdims=True)
    to_table = pltpu.make_async_copy(pointers, table, table_sem.at[0])
    to_table.start()
    own[...] = jnp.zeros_like(own)
    for k in range(depth):
        slots[k, 0] = jnp.zeros((hours, width), jnp.float32)

    pl.semaphore_wait(barrier, n - 1)

    starts = []
    for k, other in enumerate(everyone):
        copy = remote(
            base_row_ref.at[:, pl.ds(pl.multiple_of(other * reach, reach), reach)], rows.at[me],
            start_send.at[0, k], start_recv.at[0, k], other,
        )
        copy.start()
        starts.append(copy)
    levels = []
    for k, other in enumerate(everyone):
        copy = remote(soc_ref, level_recv.at[me], start_send.at[1, k], start_recv.at[1, k], other)
        copy.start()
        levels.append(copy)
    rows[me] = base_row_ref[:, pl.ds(pl.multiple_of(me * reach, reach), reach)]
    level_recv[me] = soc_ref[...]
    to_table.wait()
    for copy in starts:
        copy.wait()
    for h in range(n):
        row = rows[h].astype(jnp.float32)
        for b in range(blocks):
            base[b, h:h + 1, :] = row[:, b * width:(b + 1) * width]
    inj[...] = base[...]
    sent[...] = base[...].astype(sent.dtype)

    def product(it, k, other, out):
        first = owner(k, other) * own_groups
        for g in range(own_groups):
            picked = jnp.concatenate([sent[block_ref[t, first + g]] for t in range(depth)], axis=1)
            wide = jnp.concatenate([held[first + g, t] for t in range(depth)], axis=1)
            out[it, k, g * hours:(g + 1) * hours] = lax.dot_general(
                picked, wide, (((1,), (1,)), ((), ())), preferred_element_type=jnp.float32
            )

    def pair(it, k):
        return remote(
            theirs.at[it, k], first_recv.at[it, k], pair_send.at[it, k], pair_recv.at[it, k], partner
        )

    def row(it, k):
        return remote(
            first_sum.at[it, k], second_recv.at[it, k], row_send.at[it, k], row_recv.at[it, k],
            lax.rem(spot + k + 1, half) * 2 + core,
        )

    def far_copy(it, k):
        chunk = all_dual.at[it, me]
        device = lax.rem(far + k + 1, quarter) * 4 + lane
        return remote(chunk, chunk, far_send.at[it, k], far_recv.at[it, k], device)

    def mid_copy(it, k):
        chunk = all_dual.at[it, chunk_at(k)]
        return remote(chunk, chunk, mid_send.at[it, k], mid_recv.at[it, k], across)

    def near_copy(it, k):
        chunk = all_dual.at[it, chunk_at(k)]
        return remote(chunk, chunk, near_send.at[it, k], near_recv.at[it, k], partner)

    def pass_on(it, k):
        pair(it, k).wait_recv()
        first_sum[it, k] = (mine[it, k] + first_recv[it, k]).astype(jnp.bfloat16)
        row(it, k).start()

    def add_price(it, pos):
        chunk = chunk_at(pos)
        for g in range(own_groups):
            group = chunk * own_groups + g
            place = pos * own_groups + g + 1
            wide = jnp.concatenate([held[group, k] for k in range(depth)], axis=1)
            part = jnp.dot(
                all_dual[it, chunk, g * hours:(g + 1) * hours], wide, preferred_element_type=jnp.float32
            )
            for k in range(depth):
                slots[k, place] = slots[k, table[k, group]] + part[:, k * width:(k + 1) * width]

    def loop(count, body):
        def step(k, carry):
            body(k)
            return carry

        lax.fori_loop(0, count, step, 0)

    def update():
        for r in range(blocks):
            total = slots[0, table[depth, r]]
            for k in range(1, depth):
                total = total + slots[k, table[depth + k, r]]
            price[r] = total
        flat = price[...].astype(jnp.bfloat16).reshape(blocks * hours, width)
        moved = jnp.zeros((blocks * hours, width), jnp.float32)
        for start in range(0, units, unit_chunk):
            part = pl.ds(start, unit_chunk)
            bus = bus_ref[:, part]
            block = jnp.broadcast_to(lax.div(bus, width) - me * blocks, (hours, unit_chunk))
            spots = lax.broadcasted_iota(jnp.int32, (width, unit_chunk), 0)
            chosen = jnp.where(spots == lax.rem(bus, width), 1.0, 0.0).astype(jnp.bfloat16)
            now = level[:, part]
            before = pltpu.roll(now, 1, 0)
            charge = now - before
            spread = jnp.concatenate(
                [jnp.where(block == r, charge, 0.0).astype(jnp.bfloat16) for r in range(blocks)], axis=0
            )
            moved = moved + lax.dot_general(
                spread, chosen, (((1,), (1,)), ((), ())), preferred_element_type=jnp.float32
            )
            found = jnp.dot(flat, chosen, preferred_element_type=jnp.float32)
            store_price = jnp.zeros_like(now)
            for r in range(blocks):
                store_price = store_price + jnp.where(block == r, found[r * hours:(r + 1) * hours], 0.0)
            level[:, part] = 0.5 * (now + before) - gain_ref[:, part] * store_price
        for r in range(blocks):
            now = inj[r]
            ramp = 2.0 * now - pltpu.roll(now, 1, 0) - pltpu.roll(now, hours - 1, 0)
            updated = now - step_size * ((now - base[r]) + penalty * price[r] + ramp_weight * ramp)
            updated = updated - step_size * moved[r * hours:(r + 1) * hours]
            inj[r] = updated
            sent[r] = updated.astype(jnp.bfloat16)

    def iteration(it):
        def flow_step(k):
            for other, out in ((True, theirs), (False, mine)):
                @pl.when(it == 0)
                def _():
                    fetch(k, other).wait()

                product(it, k, other, out)
                if other:
                    pair(it, k).start()

            @pl.when(k >= 1)
            def _():
                pass_on(it, k - 1)

        loop(half, flow_step)

        @pl.when(it == 0)
        def _():
            for copy in levels:
                copy.wait()
            for h in range(n):
                level[h:h + 1, :] = level_recv[h]

        pair(it, half - 1).wait_recv()
        total = mine[it, half - 1] + first_recv[it, half - 1] + own[...]
        for k in range(half - 1):
            row(it, k).wait_recv()
            total = total + second_recv[it, k].astype(jnp.float32)
        shifted = total.reshape(own_groups, hours, width)
        bound = limits_ref[pl.ds(me * own_groups, own_groups), :][:, None, :]
        clipped = jnp.minimum(jnp.maximum(shifted, -bound), bound)
        dual = (shifted - clipped).reshape(total.shape)
        all_dual[it, me] = dual.astype(jnp.bfloat16)
        own[...] = dual

        for k in range(quarter - 1):
            far_copy(it, k).start()
        mid_copy(it, 0).start()
        near_copy(it, 0).start()
        add_price(it, 0)

        def far_step(k):
            far_copy(it, k).wait_recv()
            mid_copy(it, k + 1).start()
            near_copy(it, k + 1).start()
            add_price(it, k + 1)

        def mid_step(k):
            mid_copy(it, k).wait_recv()
            near_copy(it, quarter + k).start()
            add_price(it, quarter + k)

        def near_step(k):
            near_copy(it, k).wait_recv()
            add_price(it, half + k)

        loop(quarter - 1, far_step)
        loop(quarter, mid_step)
        loop(half, near_step)
        update()
        loop(quarter - 1, lambda k: far_copy(it, k).wait_send())
        loop(quarter, lambda k: mid_copy(it, k).wait_send())

        def sent_all(k):
            near_copy(it, k).wait_send()
            pair(it, k).wait_send()

        loop(half, sent_all)
        loop(half - 1, lambda k: row(it, k).wait_send())

    loop(ITERS, iteration)

    for r in range(blocks):
        now = inj[r]
        for h in range(hours):
            inj_rows[h, :, r * width:(r + 1) * width] = now[h:h + 1]
    for g in range(own_groups):
        now = own[g * hours:(g + 1) * hours]
        for h in range(hours):
            dual_rows[h, :, g * width:(g + 1) * width] = now[h:h + 1]
    block = lax.div(bus_ref[...], width) - me * blocks
    kept = jnp.where((block >= 0) & (block < blocks), level[...], 0.0)
    for q in range(units // width):
        level_parts[:, q, :] = kept[:, q * width:(q + 1) * width]
    level_rows[...] = level_parts[...].astype(level_rows.dtype)
    inj_here = inj_out.at[:, pl.ds(pl.multiple_of(me * reach, reach), reach)]
    dual_here = dual_out.at[:, pl.ds(pl.multiple_of(me * span, span), span)]
    ends = []
    for k, other in enumerate(everyone):
        for part, (src, dst) in enumerate((
            (inj_rows.at[other], inj_here),
            (dual_rows.at[other], dual_here),
            (level_rows.at[other], level_last.at[k]),
        )):
            copy = remote(src, dst, end_send.at[part, k], end_recv.at[part, k], other)
            copy.start()
            ends.append(copy)
    inj_here[...] = inj_rows[me]
    dual_here[...] = dual_rows[me]
    for copy in ends:
        copy.wait()
    result = level_parts[me]
    for k in range(n - 1):
        result = result + level_last[k].astype(jnp.float32)
    level_out[...] = result


def admm(n, table, base_row, limits, unit_bus, gain, soc, tiles):
    half, quarter = n // 2, n // 4
    groups, depth, lines, width = tiles.shape
    hours = n
    blocks = base_row.shape[1] // n // width
    own_groups = groups // n
    units = soc.shape[1]
    chunk = (own_groups * hours, lines)
    grid = (blocks, hours, width)
    parts = (hours, units // width, width)
    dma = pltpu.SemaphoreType.DMA
    f32, bf16 = jnp.float32, jnp.bfloat16
    return pl.pallas_call(
        functools.partial(admm_kernel, n, 512 if units % 512 == 0 else units),
        out_shape=(
            jax.ShapeDtypeStruct(base_row.shape, f32),
            jax.ShapeDtypeStruct((1, groups * lines), f32),
            jax.ShapeDtypeStruct(parts[1:], f32),
        ),
        in_specs=[pl.BlockSpec(memory_space=pltpu.SMEM)] + [VM] * 6 + [pl.BlockSpec(memory_space=pl.ANY)],
        out_specs=(VM,) * 3,
        scratch_shapes=[
            pltpu.VMEM(tiles.shape, tiles.dtype),
            pltpu.VMEM((n, 1, blocks * width), bf16),
            pltpu.VMEM(grid, f32), pltpu.VMEM(grid, f32), pltpu.VMEM(grid, bf16), pltpu.VMEM(grid, f32),
            pltpu.VMEM((n, 1, units), f32),
            pltpu.VMEM((hours, units), f32),
            pltpu.VMEM((2 * depth, groups), jnp.int32),
            pltpu.SMEM((2 * depth, groups), jnp.int32),
            pltpu.VMEM((ITERS, half) + chunk, f32),
            pltpu.VMEM((ITERS, half) + chunk, f32),
            pltpu.VMEM((ITERS, half) + chunk, f32),
            pltpu.VMEM((ITERS, half - 1) + chunk, bf16),
            pltpu.VMEM((ITERS, half - 1) + chunk, bf16),
            pltpu.VMEM(chunk, f32),
            pltpu.VMEM((ITERS, n) + chunk, bf16),
            pltpu.VMEM((depth, groups + 1, hours, width), f32),
            pltpu.VMEM((hours, 1, blocks * width), f32),
            pltpu.VMEM((hours, 1, own_groups * lines), f32),
            pltpu.VMEM(parts, bf16),
            pltpu.VMEM(parts, f32),
            pltpu.VMEM((n - 1,) + parts[1:], bf16),
            dma((n,)), dma((1,)),
            dma((2, n - 1)), dma((2, n - 1)),
            dma((ITERS, half)), dma((ITERS, half)),
            dma((ITERS, half - 1)), dma((ITERS, half - 1)),
            dma((ITERS, quarter - 1)), dma((ITERS, quarter - 1)),
            dma((ITERS, quarter)), dma((ITERS, quarter)),
            dma((ITERS, half)), dma((ITERS, half)),
            dma((3, n - 1)), dma((3, n - 1)),
        ],
        compiler_params=pltpu.CompilerParams(collective_id=0, has_side_effects=True),
        name="admm",
    )(table, table, base_row, limits, unit_bus, gain, soc, tiles)


def finish_kernel(*refs):
    count = len(refs) // 2
    for src, dst in zip(refs[:count], refs[count:]):
        dst[...] = src[...]


def finish(*arrays):
    return pl.pallas_call(
        finish_kernel,
        out_shape=tuple(jax.ShapeDtypeStruct(a.shape, a.dtype) for a in arrays),
        in_specs=[VM] * len(arrays),
        out_specs=(VM,) * len(arrays),
        name="finish",
    )(*arrays)


def shards(base_injection, ptdf_tiles, tile_block, limits, stor_bus, stor_gain, soc_init):
    n = lax.axis_size("tm")
    groups, _, lines, width = ptdf_tiles.shape
    units = soc_init.shape[1]
    inj, dual, level = admm(
        n, tile_block.T, base_injection, limits.reshape(groups, lines), stor_bus.reshape(1, units),
        stor_gain.reshape(1, units), soc_init, ptdf_tiles,
    )
    inj, dual, level = finish(inj.reshape(-1, width), dual.reshape(-1, lines), level)
    return inj.reshape(1, -1), dual.reshape(1, -1), level.reshape(1, -1)


def solution(mesh):
    in_specs = (
        P(("scen", "tm"), None),
        P(None, "tm", None, None),
        P(None, "tm"),
        P(),
        P(),
        P(),
        P(("scen", "tm"), None),
    )
    out_specs = (P(("scen", "tm"), None), P(("scen", "tm"), None), P(("scen", "tm"), None))
    return jax.shard_map(shards, mesh=mesh, in_specs=in_specs, out_specs=out_specs, check_vma=False)
```

```python
import functools

import jax
import jax.numpy as jnp
from jax import lax
from jax.experimental import pallas as pl
from jax.experimental.pallas import tpu as pltpu
from jax.sharding import PartitionSpec as P

ITERS = 2

step_size = 0.5
penalty = 4.0
ramp_weight = 0.5

VM = pl.BlockSpec(memory_space=pltpu.VMEM)
MESH = pl.DeviceIdType.MESH


def admm_kernel(
    n, unit_chunk, block_ref, block_rows_ref, base_row_ref, limits_ref, bus_ref, gain_ref, soc_ref, tiles_ref,
    ends_out, dual_out,
    held, rows, base, inj, sent, price, level_recv, level, pointers, table,
    theirs, mine, first_recv, first_sum, second_recv, own, all_dual, slots, moved, end_wide, end_rows,
    tile_sem, table_sem, start_send, start_recv, pair_send, pair_recv, row_send, row_recv,
    far_send, far_recv, mid_send, mid_recv, near_send, near_recv, end_send, end_recv,
):
    half, quarter = n // 2, n // 4
    groups, depth, _, width = held.shape
    blocks, hours = base.shape[:2]
    reach = blocks * width
    own_groups = groups // n
    units = level.shape[1]
    me = lax.axis_index("tm")
    core = lax.rem(me, 2)
    side = lax.rem(me // 2, 2)
    spot = me // 2
    far, lane = me // 4, lax.rem(me, 4)
    partner = me + 1 - 2 * core
    across = me + 2 - 4 * side
    everyone = [lax.rem(me + k, n) for k in range(1, n)]

    def remote(src, dst, send, recv, device):
        return pltpu.make_async_remote_copy(
            src_ref=src, dst_ref=dst, send_sem=send, recv_sem=recv,
            device_id={"tm": device}, device_id_type=MESH,
        )

    def owner(k, other):
        return lax.rem(spot + k + 1, half) * 2 + (1 - core if other else core)

    def fetch(k):
        place = pl.ds(lax.rem(spot + k + 1, half) * 2 * own_groups, 2 * own_groups)
        return pltpu.make_async_copy(tiles_ref.at[place], held.at[place], tile_sem.at[k])

    def chunk_at(pos):
        z = lax.rem(far + quarter - lax.rem(pos, quarter), quarter)
        y = lax.rem(side + lax.rem(pos // quarter, 2), 2)
        c = lax.rem(core + pos // half, 2)
        return z * 4 + y * 2 + c

    for k in range(half):
        fetch(k).start()

    barrier = pltpu.get_barrier_semaphore()
    for other in everyone:
        pl.semaphore_signal(barrier, inc=1, device_id={"tm": other}, device_id_type=MESH)

    group_pos = []
    for dim in (0, 1):
        g = lax.broadcasted_iota(jnp.int32, (groups, groups), dim)
        dev = lax.div(g, own_groups)
        turn = lax.rem(far + quarter - lax.div(dev, 4), quarter)
        other_side = lax.rem(lax.rem(lax.div(dev, 2), 2) + side, 2)
        other_core = lax.rem(lax.rem(dev, 2) + core, 2)
        pos = (other_core * half + other_side * quarter + turn) * own_groups + lax.rem(g, own_groups)
        group_pos.append(pos)
    down, along = group_pos
    numbers = lax.broadcasted_iota(jnp.int32, (groups, groups), 1)
    for k in range(depth):
        here = jnp.broadcast_to(block_rows_ref[k:k + 1, :], (groups, groups))
        there = here.T
        before = jnp.where((here == there) & (down < along), down + 1, 0)
        pointers[k:k + 1, :] = jnp.max(before, axis=0, keepdims=True)
        final = jnp.where(there == numbers, down + 1, 0)
        pointers[depth + k:depth + k + 1, :] = jnp.max(final, axis=0, keepdims=True)
    to_table = pltpu.make_async_copy(pointers, table, table_sem.at[0])
    to_table.start()
    own[...] = jnp.zeros_like(own)
    end_wide[...] = jnp.zeros_like(end_wide)
    for k in range(depth):
        slots[k, 0] = jnp.zeros((hours, width), jnp.float32)

    pl.semaphore_wait(barrier, n - 1)

    for other in everyone:
        remote(
            base_row_ref.at[:, pl.ds(pl.multiple_of(other * reach, reach), reach)], rows.at[me],
            start_send.at[0], start_recv.at[0], other,
        ).start()
    for other in everyone:
        remote(soc_ref, level_recv.at[me], start_send.at[1], start_recv.at[1], other).start()
    others = pl.ds(0, n - 1)
    starts = remote(rows.at[others], rows.at[others], start_send.at[0], start_recv.at[0], partner)
    levels = remote(level_recv.at[others], level_recv.at[others], start_send.at[1], start_recv.at[1], partner)
    rows[me] = base_row_ref[:, pl.ds(pl.multiple_of(me * reach, reach), reach)]
    level_recv[me] = soc_ref[...]
    to_table.wait()
    starts.wait()
    for h in range(n):
        row = rows[h].astype(jnp.float32)
        for b in range(blocks):
            base[b, h:h + 1, :] = row[:, b * width:(b + 1) * width]
    inj[...] = base[...]
    sent[...] = base[...].astype(sent.dtype)

    def product(it, k, other, out):
        first = owner(k, other) * own_groups
        for g in range(own_groups):
            picked = jnp.concatenate([sent[block_ref[t, first + g]] for t in range(depth)], axis=1)
            wide = jnp.concatenate([held[first + g, t] for t in range(depth)], axis=1)
            out[it, k, g * hours:(g + 1) * hours] = lax.dot_general(
                picked, wide, (((1,), (1,)), ((), ())), preferred_element_type=jnp.float32
            )

    def pair(it, k):
        return remote(
            theirs.at[it, k], first_recv.at[it, k], pair_send.at[0], pair_recv.at[it, k], partner
        )

    def row(it, k):
        return remote(
            first_sum.at[it, k], second_recv.at[it, k], row_send.at[0], row_recv.at[it],
            lax.rem(spot + k + 1, half) * 2 + core,
        )

    def far_copy(it, k):
        chunk = all_dual.at[it, me]
        device = lax.rem(far + k + 1, quarter) * 4 + lane
        return remote(chunk, chunk, far_send.at[0], far_recv.at[it, k], device)

    def mid_copy(it, k):
        chunk = all_dual.at[it, chunk_at(k)]
        return remote(chunk, chunk, mid_send.at[0], mid_recv.at[it, k], across)

    def near_copy(it, k):
        chunk = all_dual.at[it, chunk_at(k)]
        return remote(chunk, chunk, near_send.at[0], near_recv.at[it, k], partner)

    def pass_on(it, k):
        pair(it, k).wait_recv()
        first_sum[it, k] = (mine[it, k] + first_recv[it, k]).astype(jnp.bfloat16)
        row(it, k).start()

    def add_price(it, pos):
        chunk = chunk_at(pos)
        for g in range(own_groups):
            group = chunk * own_groups + g
            place = pos * own_groups + g + 1
            wide = jnp.concatenate([held[group, k] for k in range(depth)], axis=1)
            part = jnp.dot(
                all_dual[it, chunk, g * hours:(g + 1) * hours], wide, preferred_element_type=jnp.float32
            )
            for k in range(depth):
                slots[k, place] = slots[k, table[k, group]] + part[:, k * width:(k + 1) * width]

    def loop(count, body):
        def step(k, carry):
            body(k)
            return carry

        lax.fori_loop(0, count, step, 0)

    def unit_part(start):
        part = pl.ds(start, unit_chunk)
        bus = bus_ref[:, part]
        block = jnp.broadcast_to(lax.div(bus, width) - me * blocks, (hours, unit_chunk))
        spots = lax.broadcasted_iota(jnp.int32, (width, unit_chunk), 0)
        chosen = jnp.where(spots == lax.rem(bus, width), 1.0, 0.0).astype(jnp.bfloat16)
        return part, block, chosen

    def move_charges():
        total = jnp.zeros((blocks * hours, width), jnp.float32)
        for start in range(0, units, unit_chunk):
            part, block, chosen = unit_part(start)
            now = level[:, part]
            charge = now - pltpu.roll(now, 1, 0)
            spread = jnp.concatenate(
                [jnp.where(block == r, charge, 0.0).astype(jnp.bfloat16) for r in range(blocks)], axis=0
            )
            total = total + lax.dot_general(
                spread, chosen, (((1,), (1,)), ((), ())), preferred_element_type=jnp.float32
            )
        moved[...] = total

    def update():
        for r in range(blocks):
            total = slots[0, table[depth, r]]
            for k in range(1, depth):
                total = total + slots[k, table[depth + k, r]]
            price[r] = total
        flat = price[...].astype(jnp.bfloat16).reshape(blocks * hours, width)
        for start in range(0, units, unit_chunk):
            part, block, chosen = unit_part(start)
            now = level[:, part]
            found = jnp.dot(flat, chosen, preferred_element_type=jnp.float32)
            store_price = jnp.zeros_like(now)
            for r in range(blocks):
                store_price = store_price + jnp.where(block == r, found[r * hours:(r + 1) * hours], 0.0)
            level[:, part] = 0.5 * (now + pltpu.roll(now, 1, 0)) - gain_ref[:, part] * store_price
        for r in range(blocks):
            now = inj[r]
            ramp = 2.0 * now - pltpu.roll(now, 1, 0) - pltpu.roll(now, hours - 1, 0)
            updated = now - step_size * ((now - base[r]) + penalty * price[r] + ramp_weight * ramp)
            updated = updated - step_size * moved[r * hours:(r + 1) * hours]
            inj[r] = updated
            sent[r] = updated.astype(jnp.bfloat16)

    def iteration(it):
        def flow_step(k):
            @pl.when(it == 0)
            def _():
                fetch(k).wait()

            product(it, k, True, theirs)
            product(it, k, False, mine)
            pair(it, k).start()

            @pl.when(k >= 1)
            def _():
                pass_on(it, k - 1)

        loop(half, flow_step)

        @pl.when(it == 0)
        def _():
            levels.wait()
            for h in range(n):
                level[h:h + 1, :] = level_recv[h]

        pair(it, half - 1).wait_recv()
        total = mine[it, half - 1] + first_recv[it, half - 1] + own[...]
        remote(
            first_sum.at[it], second_recv.at[it], row_send.at[0], row_recv.at[it], partner
        ).wait_recv()
        for k in range(half - 1):
            total = total + second_recv[it, k].astype(jnp.float32)
        shifted = total.reshape(own_groups, hours, width)
        bound = limits_ref[pl.ds(me * own_groups, own_groups), :][:, None, :]
        clipped = jnp.minimum(jnp.maximum(shifted, -bound), bound)
        dual = (shifted - clipped).reshape(total.shape)
        all_dual[it, me] = dual.astype(jnp.bfloat16)
        own[...] = dual

        for k in range(quarter - 1):
            far_copy(it, k).start()
        mid_copy(it, 0).start()
        near_copy(it, 0).start()
        add_price(it, 0)
        move_charges()

        def far_step(k):
            far_copy(it, k).wait_recv()
            mid_copy(it, k + 1).start()
            near_copy(it, k + 1).start()
            add_price(it, k + 1)

        def mid_step(k):
            mid_copy(it, k).wait_recv()
            near_copy(it, quarter + k).start()
            add_price(it, quarter + k)

        def near_step(k):
            near_copy(it, k).wait_recv()
            add_price(it, half + k)

        loop(quarter - 1, far_step)
        loop(quarter, mid_step)
        loop(half, near_step)
        update()
        for buffer, sem, count in (
            (all_dual, far_send, quarter - 1), (all_dual, mid_send, quarter), (all_dual, near_send, half),
            (theirs, pair_send, half), (first_sum, row_send, half - 1),
        ):
            whole = buffer.at[it, pl.ds(0, count)]
            remote(whole, whole, sem.at[0], row_recv.at[it], partner).wait_send()

    loop(ITERS, iteration)

    for r in range(blocks):
        end_wide[:, r, :] = inj[r]
    block = lax.div(bus_ref[...], width) - me * blocks
    kept = jnp.where((block >= 0) & (block < blocks), level[...], 0.0)
    for q in range(units // width):
        end_wide[:, blocks + q, :] = kept[:, q * width:(q + 1) * width]
    end_rows[...] = end_wide[...].astype(end_rows.dtype)
    for other in everyone:
        remote(end_rows.at[other], ends_out.at[me], end_send.at[0], end_recv.at[0], other).start()
    ends_out[me] = end_rows[me]
    hour = lax.broadcasted_iota(jnp.int32, (own_groups, hours, width), 1)
    for c in range(n):
        dual = all_dual[ITERS - 1, c].astype(jnp.float32).reshape(own_groups, hours, width)
        dual_out[c * own_groups:(c + 1) * own_groups, :] = jnp.sum(jnp.where(hour == me, dual, 0.0), axis=1)
    remote(end_rows.at[others], ends_out.at[others], end_send.at[0], end_recv.at[0], partner).wait()


def admm(n, table, base_row, limits, unit_bus, gain, soc, tiles):
    half, quarter = n // 2, n // 4
    groups, depth, lines, width = tiles.shape
    hours = n
    blocks = base_row.shape[1] // n // width
    own_groups = groups // n
    units = soc.shape[1]
    chunk = (own_groups * hours, lines)
    grid = (blocks, hours, width)
    ends = (hours, pl.cdiv(blocks + units // width, 8) * 8, width)
    dma = pltpu.SemaphoreType.DMA
    f32, bf16 = jnp.float32, jnp.bfloat16
    return pl.pallas_call(
        functools.partial(admm_kernel, n, 512 if units % 512 == 0 else units),
        out_shape=(
            jax.ShapeDtypeStruct(ends, bf16),
            jax.ShapeDtypeStruct((groups, lines), f32),
        ),
        in_specs=[pl.BlockSpec(memory_space=pltpu.SMEM)] + [VM] * 6 + [pl.BlockSpec(memory_space=pl.ANY)],
        out_specs=(VM,) * 2,
        scratch_shapes=[
            pltpu.VMEM(tiles.shape, tiles.dtype),
            pltpu.VMEM((n, 1, blocks * width), bf16),
            pltpu.VMEM(grid, f32), pltpu.VMEM(grid, f32), pltpu.VMEM(grid, bf16), pltpu.VMEM(grid, f32),
            pltpu.VMEM((n, 1, units), f32),
            pltpu.VMEM((hours, units), f32),
            pltpu.VMEM((2 * depth, groups), jnp.int32),
            pltpu.SMEM((2 * depth, groups), jnp.int32),
            pltpu.VMEM((ITERS, half) + chunk, f32),
            pltpu.VMEM((ITERS, half) + chunk, f32),
            pltpu.VMEM((ITERS, half) + chunk, f32),
            pltpu.VMEM((ITERS, half - 1) + chunk, bf16),
            pltpu.VMEM((ITERS, half - 1) + chunk, bf16),
            pltpu.VMEM(chunk, f32),
            pltpu.VMEM((ITERS, n) + chunk, bf16),
            pltpu.VMEM((depth, groups + 1, hours, width), f32),
            pltpu.VMEM((blocks * hours, width), f32),
            pltpu.VMEM(ends, f32),
            pltpu.VMEM(ends, bf16),
            dma((half,)), dma((1,)), dma((2,)), dma((2,)),
            dma((1,)), dma((ITERS, half)),
            dma((1,)), dma((ITERS,)),
            dma((1,)), dma((ITERS, quarter - 1)),
            dma((1,)), dma((ITERS, quarter)),
            dma((1,)), dma((ITERS, half)),
            dma((1,)), dma((1,)),
        ],
        compiler_params=pltpu.CompilerParams(collective_id=0, has_side_effects=True),
        name="admm",
    )(table, table, base_row, limits, unit_bus, gain, soc, tiles)


def finish_kernel(ends_ref, dual_ref, inj_out, dual_out, level_out):
    count = ends_ref.shape[0]
    blocks = inj_out.shape[0] // count
    own = level_out.shape[0]
    total = jnp.zeros(level_out.shape, jnp.float32)
    for d in range(count):
        part = ends_ref[d].astype(jnp.float32)
        inj_out[d * blocks:(d + 1) * blocks, :] = part[:blocks]
        total = total + part[blocks:blocks + own]
    level_out[...] = total
    dual_out[...] = dual_ref[...]


def finish(ends, dual, buses, units):
    width = ends.shape[2]
    f32 = jnp.float32
    return pl.pallas_call(
        finish_kernel,
        out_shape=(
            jax.ShapeDtypeStruct((buses // width, width), f32),
            jax.ShapeDtypeStruct(dual.shape, f32),
            jax.ShapeDtypeStruct((units // width, width), f32),
        ),
        in_specs=[VM] * 2,
        out_specs=(VM,) * 3,
        name="finish",
    )(ends, dual)


def shards(base_injection, ptdf_tiles, tile_block, limits, stor_bus, stor_gain, soc_init):
    n = lax.axis_size("tm")
    groups, _, lines, _ = ptdf_tiles.shape
    units = soc_init.shape[1]
    ends, dual = admm(
        n, tile_block.T, base_injection, limits.reshape(groups, lines), stor_bus.reshape(1, units),
        stor_gain.reshape(1, units), soc_init, ptdf_tiles,
    )
    inj, dual, level = finish(ends, dual, base_injection.shape[1], units)
    return inj.reshape(1, -1), dual.reshape(1, -1), level.reshape(1, -1)


def solution(mesh):
    in_specs = (
        P(("scen", "tm"), None),
        P(None, "tm", None, None),
        P(None, "tm"),
        P(),
        P(),
        P(),
        P(("scen", "tm"), None),
    )
    out_specs = (P(("scen", "tm"), None), P(("scen", "tm"), None), P(("scen", "tm"), None))
    return jax.shard_map(shards, mesh=mesh, in_specs=in_specs, out_specs=out_specs, check_vma=False)
```

```python
import functools

import jax
import jax.numpy as jnp
from jax import lax
from jax.experimental import pallas as pl
from jax.experimental.pallas import tpu as pltpu
from jax.sharding import PartitionSpec as P

ITERS = 2

step_size = 0.5
penalty = 4.0
ramp_weight = 0.5

VM = pl.BlockSpec(memory_space=pltpu.VMEM)
MESH = pl.DeviceIdType.MESH


def admm_kernel(
    n, unit_chunk, block_ref, block_rows_ref, base_row_ref, limits_ref, bus_ref, gain_ref, soc_ref, tiles_ref,
    ends_out, dual_out,
    held, rows, base, inj, sent, price, level_recv, level, pointers, table,
    theirs, mine, first_recv, first_sum, second_recv, own, all_dual, slots, moved, end_wide, end_rows,
    tile_sem, table_sem, start_send, start_recv, pair_send, pair_recv, row_send, row_recv,
    far_send, far_recv, mid_send, mid_recv, near_send, near_recv, end_send, end_recv,
):
    half, quarter = n // 2, n // 4
    groups, depth, _, width = held.shape
    blocks, hours = base.shape[:2]
    reach = blocks * width
    own_groups = groups // n
    units = level.shape[1]
    me = lax.axis_index("tm")
    core = lax.rem(me, 2)
    side = lax.rem(me // 2, 2)
    spot = me // 2
    far, lane = me // 4, lax.rem(me, 4)
    partner = me + 1 - 2 * core
    across = me + 2 - 4 * side
    everyone = [lax.rem(me + k, n) for k in range(1, n)]

    def remote(src, dst, send, recv, device):
        return pltpu.make_async_remote_copy(
            src_ref=src, dst_ref=dst, send_sem=send, recv_sem=recv,
            device_id={"tm": device}, device_id_type=MESH,
        )

    def owner(k, other):
        return lax.rem(spot + k + 1, half) * 2 + (1 - core if other else core)

    def fetch(k):
        place = pl.ds(lax.rem(spot + k + 1, half) * 2 * own_groups, 2 * own_groups)
        return pltpu.make_async_copy(tiles_ref.at[place], held.at[place], tile_sem.at[k])

    def chunk_at(pos):
        z = lax.rem(far + quarter - lax.rem(pos, quarter), quarter)
        y = lax.rem(side + lax.rem(pos // quarter, 2), 2)
        c = lax.rem(core + pos // half, 2)
        return z * 4 + y * 2 + c

    for k in range(half):
        fetch(k).start()

    barrier = pltpu.get_barrier_semaphore()
    for other in everyone:
        pl.semaphore_signal(barrier, inc=1, device_id={"tm": other}, device_id_type=MESH)

    group_pos = []
    for dim in (0, 1):
        g = lax.broadcasted_iota(jnp.int32, (groups, groups), dim)
        dev = lax.div(g, own_groups)
        turn = lax.rem(far + quarter - lax.div(dev, 4), quarter)
        other_side = lax.rem(lax.rem(lax.div(dev, 2), 2) + side, 2)
        other_core = lax.rem(lax.rem(dev, 2) + core, 2)
        pos = (other_core * half + other_side * quarter + turn) * own_groups + lax.rem(g, own_groups)
        group_pos.append(pos)
    down, along = group_pos
    numbers = lax.broadcasted_iota(jnp.int32, (groups, groups), 1)
    for k in range(depth):
        here = jnp.broadcast_to(block_rows_ref[k:k + 1, :], (groups, groups))
        there = here.T
        before = jnp.where((here == there) & (down < along), down + 1, 0)
        pointers[k:k + 1, :] = jnp.max(before, axis=0, keepdims=True)
        final = jnp.where(there == numbers, down + 1, 0)
        pointers[depth + k:depth + k + 1, :] = jnp.max(final, axis=0, keepdims=True)
    to_table = pltpu.make_async_copy(pointers, table, table_sem.at[0])
    to_table.start()
    own[...] = jnp.zeros_like(own)
    end_wide[...] = jnp.zeros_like(end_wide)
    for k in range(depth):
        slots[k, 0] = jnp.zeros((hours, width), jnp.float32)

    pl.semaphore_wait(barrier, n - 1)

    for other in everyone:
        remote(
            base_row_ref.at[:, pl.ds(pl.multiple_of(other * reach, reach), reach)], rows.at[me],
            start_send.at[0], start_recv.at[0], other,
        ).start()
    for other in everyone:
        remote(soc_ref, level_recv.at[me], start_send.at[1], start_recv.at[1], other).start()
    others = pl.ds(0, n - 1)
    starts = remote(rows.at[others], rows.at[others], start_send.at[0], start_recv.at[0], partner)
    levels = remote(level_recv.at[others], level_recv.at[others], start_send.at[1], start_recv.at[1], partner)
    rows[me] = base_row_ref[:, pl.ds(pl.multiple_of(me * reach, reach), reach)]
    level_recv[me] = soc_ref[...]
    to_table.wait()
    starts.wait()
    for h in range(n):
        row = rows[h].astype(jnp.float32)
        for b in range(blocks):
            base[b, h:h + 1, :] = row[:, b * width:(b + 1) * width]
    inj[...] = base[...]
    sent[...] = base[...].astype(sent.dtype)

    def product(it, k, other, out):
        first = owner(k, other) * own_groups
        for g in range(own_groups):
            picked = jnp.concatenate([sent[block_ref[t, first + g]] for t in range(depth)], axis=1)
            wide = jnp.concatenate([held[first + g, t] for t in range(depth)], axis=1)
            out[it, k, g * hours:(g + 1) * hours] = lax.dot_general(
                picked, wide, (((1,), (1,)), ((), ())), preferred_element_type=jnp.float32
            )

    def pair(it, k):
        return remote(
            theirs.at[it, k], first_recv.at[it, k], pair_send.at[0], pair_recv.at[it, k], partner
        )

    def row(it, k):
        return remote(
            first_sum.at[it, k], second_recv.at[it, k], row_send.at[0], row_recv.at[it],
            lax.rem(spot + k + 1, half) * 2 + core,
        )

    def far_copy(it, k):
        chunk = all_dual.at[it, me]
        device = lax.rem(far + k + 1, quarter) * 4 + lane
        return remote(chunk, chunk, far_send.at[0], far_recv.at[it, k], device)

    def mid_copy(it, k):
        chunk = all_dual.at[it, chunk_at(k)]
        return remote(chunk, chunk, mid_send.at[0], mid_recv.at[it, k], across)

    def near_copy(it, k):
        chunk = all_dual.at[it, chunk_at(k)]
        return remote(chunk, chunk, near_send.at[0], near_recv.at[it, k], partner)

    def pass_on(it, k):
        pair(it, k).wait_recv()
        first_sum[it, k] = (mine[it, k] + first_recv[it, k]).astype(jnp.bfloat16)
        row(it, k).start()

    def add_price(it, pos):
        chunk = chunk_at(pos)
        for g in range(own_groups):
            group = chunk * own_groups + g
            place = pos * own_groups + g + 1
            wide = jnp.concatenate([held[group, k] for k in range(depth)], axis=1)
            part = jnp.dot(
                all_dual[it, chunk, g * hours:(g + 1) * hours], wide, preferred_element_type=jnp.float32
            )
            for k in range(depth):
                slots[k, place] = slots[k, table[k, group]] + part[:, k * width:(k + 1) * width]

    def loop(count, body):
        def step(k, carry):
            body(k)
            return carry

        lax.fori_loop(0, count, step, 0)

    def unit_part(start):
        part = pl.ds(start, unit_chunk)
        bus = bus_ref[:, part]
        block = jnp.broadcast_to(lax.div(bus, width) - me * blocks, (hours, unit_chunk))
        spots = lax.broadcasted_iota(jnp.int32, (width, unit_chunk), 0)
        chosen = jnp.where(spots == lax.rem(bus, width), 1.0, 0.0).astype(jnp.bfloat16)
        return part, block, chosen

    def move_charges():
        total = jnp.zeros((blocks * hours, width), jnp.float32)
        for start in range(0, units, unit_chunk):
            part, block, chosen = unit_part(start)
            now = level[:, part]
            charge = now - pltpu.roll(now, 1, 0)
            spread = jnp.concatenate(
                [jnp.where(block == r, charge, 0.0).astype(jnp.bfloat16) for r in range(blocks)], axis=0
            )
            total = total + lax.dot_general(
                spread, chosen, (((1,), (1,)), ((), ())), preferred_element_type=jnp.float32
            )
        moved[...] = total

    def update():
        for r in range(blocks):
            total = slots[0, table[depth, r]]
            for k in range(1, depth):
                total = total + slots[k, table[depth + k, r]]
            price[r] = total
        flat = price[...].astype(jnp.bfloat16).reshape(blocks * hours, width)
        for start in range(0, units, unit_chunk):
            part, block, chosen = unit_part(start)
            now = level[:, part]
            found = jnp.dot(flat, chosen, preferred_element_type=jnp.float32)
            store_price = jnp.zeros_like(now)
            for r in range(blocks):
                store_price = store_price + jnp.where(block == r, found[r * hours:(r + 1) * hours], 0.0)
            level[:, part] = 0.5 * (now + pltpu.roll(now, 1, 0)) - gain_ref[:, part] * store_price
        for r in range(blocks):
            now = inj[r]
            ramp = 2.0 * now - pltpu.roll(now, 1, 0) - pltpu.roll(now, hours - 1, 0)
            updated = now - step_size * ((now - base[r]) + penalty * price[r] + ramp_weight * ramp)
            updated = updated - step_size * moved[r * hours:(r + 1) * hours]
            inj[r] = updated
            sent[r] = updated.astype(jnp.bfloat16)

    def iteration(it):
        def flow_step(k):
            @pl.when(it == 0)
            def _():
                fetch(k).wait()

            product(it, k, True, theirs)
            product(it, k, False, mine)
            pair(it, k).start()

            @pl.when(k >= 1)
            def _():
                pass_on(it, k - 1)

        loop(half, flow_step)

        @pl.when(it == 0)
        def _():
            levels.wait()
            for h in range(n):
                level[h:h + 1, :] = level_recv[h]

        pair(it, half - 1).wait_recv()
        total = mine[it, half - 1] + first_recv[it, half - 1] + own[...]
        remote(
            first_sum.at[it], second_recv.at[it], row_send.at[0], row_recv.at[it], partner
        ).wait_recv()
        for k in range(half - 1):
            total = total + second_recv[it, k].astype(jnp.float32)
        shifted = total.reshape(own_groups, hours, width)
        bound = limits_ref[pl.ds(me * own_groups, own_groups), :][:, None, :]
        clipped = jnp.minimum(jnp.maximum(shifted, -bound), bound)
        dual = (shifted - clipped).reshape(total.shape)
        all_dual[it, me] = dual.astype(jnp.bfloat16)
        own[...] = dual

        for k in range(quarter - 1):
            far_copy(it, k).start()
        mid_copy(it, 0).start()
        near_copy(it, 0).start()
        add_price(it, 0)
        move_charges()

        def far_step(k):
            far_copy(it, k).wait_recv()
            mid_copy(it, k + 1).start()
            near_copy(it, k + 1).start()
            add_price(it, k + 1)

        def mid_step(k):
            mid_copy(it, k).wait_recv()
            near_copy(it, quarter + k).start()
            add_price(it, quarter + k)

        def near_step(k):
            for j in range(2):
                near_copy(it, 2 * k + j).wait_recv()
            for j in range(2):
                add_price(it, half + 2 * k + j)

        loop(quarter - 1, far_step)
        loop(quarter, mid_step)
        loop(half // 2, near_step)
        update()
        for buffer, sem, count in (
            (all_dual, far_send, quarter - 1), (all_dual, mid_send, quarter), (all_dual, near_send, half),
            (theirs, pair_send, half), (first_sum, row_send, half - 1),
        ):
            whole = buffer.at[it, pl.ds(0, count)]
            remote(whole, whole, sem.at[0], row_recv.at[it], partner).wait_send()

    loop(ITERS, iteration)

    for r in range(blocks):
        end_wide[:, r, :] = inj[r]
    block = lax.div(bus_ref[...], width) - me * blocks
    kept = jnp.where((block >= 0) & (block < blocks), level[...], 0.0)
    for q in range(units // width):
        end_wide[:, blocks + q, :] = kept[:, q * width:(q + 1) * width]
    end_rows[...] = end_wide[...].astype(end_rows.dtype)
    for other in everyone:
        remote(end_rows.at[other], ends_out.at[me], end_send.at[0], end_recv.at[0], other).start()
    ends_out[me] = end_rows[me]
    hour = lax.broadcasted_iota(jnp.int32, (own_groups, hours, width), 1)
    for c in range(n):
        dual = all_dual[ITERS - 1, c].astype(jnp.float32).reshape(own_groups, hours, width)
        dual_out[c * own_groups:(c + 1) * own_groups, :] = jnp.sum(jnp.where(hour == me, dual, 0.0), axis=1)
    remote(end_rows.at[others], ends_out.at[others], end_send.at[0], end_recv.at[0], partner).wait()


def admm(n, table, base_row, limits, unit_bus, gain, soc, tiles):
    half, quarter = n // 2, n // 4
    groups, depth, lines, width = tiles.shape
    hours = n
    blocks = base_row.shape[1] // n // width
    own_groups = groups // n
    units = soc.shape[1]
    chunk = (own_groups * hours, lines)
    grid = (blocks, hours, width)
    ends = (hours, pl.cdiv(blocks + units // width, 8) * 8, width)
    dma = pltpu.SemaphoreType.DMA
    f32, bf16 = jnp.float32, jnp.bfloat16
    return pl.pallas_call(
        functools.partial(admm_kernel, n, 512 if units % 512 == 0 else units),
        out_shape=(
            jax.ShapeDtypeStruct(ends, bf16),
            jax.ShapeDtypeStruct((groups, lines), f32),
        ),
        in_specs=[pl.BlockSpec(memory_space=pltpu.SMEM)] + [VM] * 6 + [pl.BlockSpec(memory_space=pl.ANY)],
        out_specs=(VM,) * 2,
        scratch_shapes=[
            pltpu.VMEM(tiles.shape, tiles.dtype),
            pltpu.VMEM((n, 1, blocks * width), bf16),
            pltpu.VMEM(grid, f32), pltpu.VMEM(grid, f32), pltpu.VMEM(grid, bf16), pltpu.VMEM(grid, f32),
            pltpu.VMEM((n, 1, units), f32),
            pltpu.VMEM((hours, units), f32),
            pltpu.VMEM((2 * depth, groups), jnp.int32),
            pltpu.SMEM((2 * depth, groups), jnp.int32),
            pltpu.VMEM((ITERS, half) + chunk, f32),
            pltpu.VMEM((ITERS, half) + chunk, f32),
            pltpu.VMEM((ITERS, half) + chunk, f32),
            pltpu.VMEM((ITERS, half - 1) + chunk, bf16),
            pltpu.VMEM((ITERS, half - 1) + chunk, bf16),
            pltpu.VMEM(chunk, f32),
            pltpu.VMEM((ITERS, n) + chunk, bf16),
            pltpu.VMEM((depth, groups + 1, hours, width), f32),
            pltpu.VMEM((blocks * hours, width), f32),
            pltpu.VMEM(ends, f32),
            pltpu.VMEM(ends, bf16),
            dma((half,)), dma((1,)), dma((2,)), dma((2,)),
            dma((1,)), dma((ITERS, half)),
            dma((1,)), dma((ITERS,)),
            dma((1,)), dma((ITERS, quarter - 1)),
            dma((1,)), dma((ITERS, quarter)),
            dma((1,)), dma((ITERS, half)),
            dma((1,)), dma((1,)),
        ],
        compiler_params=pltpu.CompilerParams(collective_id=0, has_side_effects=True),
        name="admm",
    )(table, table, base_row, limits, unit_bus, gain, soc, tiles)


def finish_kernel(ends_ref, dual_ref, inj_out, dual_out, level_out):
    count = ends_ref.shape[0]
    blocks = inj_out.shape[0] // count
    own = level_out.shape[0]
    total = jnp.zeros(level_out.shape, jnp.float32)
    for d in range(count):
        part = ends_ref[d].astype(jnp.float32)
        inj_out[d * blocks:(d + 1) * blocks, :] = part[:blocks]
        total = total + part[blocks:blocks + own]
    level_out[...] = total
    dual_out[...] = dual_ref[...]


def finish(ends, dual, buses, units):
    width = ends.shape[2]
    f32 = jnp.float32
    return pl.pallas_call(
        finish_kernel,
        out_shape=(
            jax.ShapeDtypeStruct((buses // width, width), f32),
            jax.ShapeDtypeStruct(dual.shape, f32),
            jax.ShapeDtypeStruct((units // width, width), f32),
        ),
        in_specs=[VM] * 2,
        out_specs=(VM,) * 3,
        name="finish",
    )(ends, dual)


def shards(base_injection, ptdf_tiles, tile_block, limits, stor_bus, stor_gain, soc_init):
    n = lax.axis_size("tm")
    groups, _, lines, _ = ptdf_tiles.shape
    units = soc_init.shape[1]
    ends, dual = admm(
        n, tile_block.T, base_injection, limits.reshape(groups, lines), stor_bus.reshape(1, units),
        stor_gain.reshape(1, units), soc_init, ptdf_tiles,
    )
    inj, dual, level = finish(ends, dual, base_injection.shape[1], units)
    return inj.reshape(1, -1), dual.reshape(1, -1), level.reshape(1, -1)


def solution(mesh):
    in_specs = (
        P(("scen", "tm"), None),
        P(None, "tm", None, None),
        P(None, "tm"),
        P(),
        P(),
        P(),
        P(("scen", "tm"), None),
    )
    out_specs = (P(("scen", "tm"), None), P(("scen", "tm"), None), P(("scen", "tm"), None))
    return jax.shard_map(shards, mesh=mesh, in_specs=in_specs, out_specs=out_specs, check_vma=False)
```
